32 devices in a mesh: dp: 4 (over z), seq: 8 (over y, x, core).
Axes of the slice: x: 2, y: 2, z: 4, core: 2. Of those that a mesh axis runs over, the one named last changes fastest.
Arguments:
- slide_tiles: bfloat16 [64, 256, 384], P(('dp', 'seq')), parts along dimension 0, may hold values from -6 to 6
- norm_gain: float32 [2, 384], replicated, may hold values from 0.1 to 1.9
- in_weight: bfloat16 [2, 384, 1536], replicated, may hold values from -0.3125 to 0.3125
- state_weight: bfloat16 [2, 384, 44], replicated, may hold values from -0.3125 to 0.3125
- conv_weight: float32 [2, 4, 800], replicated, may hold values from -2.5 to 2.5
- conv_bias: float32 [2, 800], replicated, may hold values from -0.5 to 0.5
- step_bias: float32 [2, 12], replicated, may hold values from -5 to -3
- decay_log: float32 [2, 12], replicated, may hold values from -8.5 to 1
- skip_gain: float32 [2, 12], replicated, may hold values from 0.5 to 1.5
- out_gain: float32 [2, 768], replicated, may hold values from 0.1 to 1.9
- out_weight: bfloat16 [2, 768, 384], replicated, may hold values from -0.21875 to 0.21875
Outputs:
- tile_out: bfloat16 [64, 256, 384], P(('dp', 'seq')), parts along dimension 0
The draws below stay inside these ranges and needn't reach their ends.
There are 4 independent parts, one for each index of `dp`. The reference program is written for one: setup_inputs(seed, part) draws one part's arguments, and reference() takes and returns one part's arrays. A program takes and returns all parts, laid end to end along the dimension named above; an argument that names none is the same for every part. Nothing has to cross between parts.
All inputs are finite; a program needn't handle non-finite values.
Results may differ from the reference program's by a relative error of at most 0.014.
Values may be sent and summed in bfloat16 or wider, within the bound.
A program may use at most 64 MiB of HBM per device.

```python
import jax
import jax.numpy as jnp
from jax import lax

D = 384
HEADS = 12
HEADDIM = 64
STATE = 16
KERNEL = 4
GROUP = 256
COLS = 256
INNER = 768
ROWS = 16


def draw_decay_log(key, part):
    values = jax.random.uniform(key, (2, HEADS), jnp.float32, -8.5, 1.0)
    return values


def shard_levels(key, dims, cuts, least, top_value):
    loudness = 1.0
    for dim, parts in cuts:
        draws = jax.random.uniform(jax.random.fold_in(jax.random.fold_in(key, 6), dim), (parts,), jnp.float32, least / len(cuts), top_value / len(cuts))
        loudness = loudness * jnp.repeat(jnp.exp(draws), dims[dim] // parts).reshape((-1,) + (1,) * (len(dims) - 1 - dim))
    return loudness


def scatter_about(own_key, dims, deviation, most, shards=(), kind=jnp.bfloat16):
    entries = jax.random.normal(own_key, dims, jnp.float32) * deviation
    if len(shards) > 0:
        entries = shard_levels(own_key, dims, shards, -0.22, 0.18) * entries
    return jnp.clip(entries, min=-most, max=most).astype(kind)


def setup_inputs(seed: int = 0, part: int = 0) -> dict:
    streams_of = jax.random.split(jax.random.key(seed), 12)
    part_splits = jax.random.split(jax.random.fold_in(streams_of[11], part), 12)
    return {
        "slide_tiles": scatter_about(part_splits[0], (ROWS, COLS, D), 1.0, 6.0, ((0, 8),)),
        "norm_gain": jnp.clip(1.0 + 0.18 * jax.random.normal(streams_of[1], (2, D), jnp.float32), 0.1, 1.9),
        "in_weight": scatter_about(streams_of[2], (2, D, 2 * INNER), D ** -0.5, 0.3125),
        "state_weight": scatter_about(streams_of[3], (2, D, 2 * STATE + HEADS), D ** -0.5, 0.3125),
        "conv_weight": scatter_about(streams_of[4], (2, KERNEL, INNER + 2 * STATE), 0.5, 2.5, (), jnp.float32),
        "conv_bias": jnp.clip(jax.random.uniform(streams_of[5], (2, INNER + 2 * STATE), jnp.float32, -0.5, 0.5), -0.5, 0.5),
        "step_bias": jnp.clip(jax.random.uniform(streams_of[6], (2, HEADS), jnp.float32, -5.0, -3.0), -5.0, -3.0),
        "decay_log": draw_decay_log(jax.random.fold_in(streams_of[11], 71), part),
        "skip_gain": jnp.clip(jax.random.uniform(streams_of[8], (2, HEADS), jnp.float32, 0.5, 1.5), 0.5, 1.5),
        "out_gain": jnp.clip(1.0 + 0.18 * jax.random.normal(streams_of[9], (2, INNER), jnp.float32), 0.1, 1.9),
        "out_weight": scatter_about(streams_of[10], (2, INNER, D), INNER ** -0.5, 0.21875),
    }


epsilon = 1e-05

def rms_scaled(values, scale_gain):
    values = values.astype(jnp.float32)
    return values * lax.rsqrt(lax.optimization_barrier(jnp.mean(values * values, axis=-1, keepdims=True)) + epsilon) * scale_gain

def group_update(carry_state, group_in):
    group_x, group_b, group_c, group_step, group_rate = group_in
    cumulative = jnp.cumsum(group_rate, axis=0)
    positions = jnp.arange(group_x.shape[0])
    lower_mask = positions[:, None] >= positions[None, :]
    cum_heads = cumulative.T
    differences = cum_heads[:, :, None] - cum_heads[:, None, :]
    decay_mask = jnp.exp(jnp.where(lower_mask[None], differences, -jnp.inf))
    scores = jnp.dot(group_c, group_b.T, preferred_element_type=jnp.float32)
    weights = (scores[None] * decay_mask * group_step.T[:, None, :]).astype(jnp.bfloat16)
    intra_out = jnp.einsum('hts,shp->thp', weights.astype(jnp.float32), group_x.astype(jnp.float32))
    inter_out = jnp.exp(cumulative)[:, :, None] * jnp.einsum('tn,hpn->thp', group_c.astype(jnp.float32), carry_state, precision=lax.Precision.HIGHEST)
    tail_weight = jnp.exp(cumulative[-1][None, :] - cumulative) * group_step
    weighted_x = (group_x.astype(jnp.float32) * tail_weight[:, :, None]).astype(jnp.bfloat16)
    local_state = jnp.einsum('shp,sn->hpn', weighted_x.astype(jnp.float32), group_b.astype(jnp.float32))
    next_state = jnp.exp(cumulative[-1])[:, None, None] * carry_state + local_state
    return (next_state, intra_out + inter_out)

def mixer(sequence, layer, norm_gain, in_weight, state_weight, conv_weight, conv_bias, step_bias, decay_log, skip_gain, out_gain):
    length = sequence.shape[0]
    inner_width = in_weight.shape[2] // 2
    normed = rms_scaled(sequence, norm_gain[layer]).astype(jnp.bfloat16)
    gate_x = jnp.dot(normed, in_weight[layer], preferred_element_type=jnp.float32).astype(jnp.bfloat16)
    state_proj = jnp.dot(normed, state_weight[layer], preferred_element_type=jnp.float32).astype(jnp.bfloat16)
    conv_in = jnp.concatenate([gate_x[:, inner_width:], state_proj[:, :2 * STATE]], axis=1)
    margin = conv_weight.shape[1] - 1
    padded = jnp.concatenate([jnp.zeros((margin, conv_in.shape[1]), jnp.bfloat16), conv_in], axis=0)
    conv_sum = jnp.zeros((length, conv_in.shape[1]), jnp.float32) + conv_bias[layer][None, :]
    for offset in range(margin + 1):
        conv_sum = conv_sum + conv_weight[layer, offset][None, :] * padded[offset:offset + length].astype(jnp.float32)
    conv_out = jax.nn.silu(conv_sum).astype(jnp.bfloat16)
    x_conv = conv_out[:, :inner_width]
    b_conv = conv_out[:, inner_width:inner_width + STATE]
    c_conv = conv_out[:, inner_width + STATE:]
    step_size = jax.nn.softplus(state_proj[:, 2 * STATE:].astype(jnp.float32) + step_bias[layer][None, :])
    log_rates = -step_size * jnp.exp(decay_log[layer])[None, :]
    group_count = length // GROUP
    inputs = (x_conv.reshape(group_count, GROUP, HEADS, HEADDIM), b_conv.reshape(group_count, GROUP, STATE), c_conv.reshape(group_count, GROUP, STATE), step_size.reshape(group_count, GROUP, HEADS), log_rates.reshape(group_count, GROUP, HEADS))
    final_state, outputs = lax.scan(group_update, jnp.zeros((HEADS, HEADDIM, STATE), jnp.float32), inputs)
    y_total = outputs.reshape(length, HEADS, HEADDIM)
    y_total = y_total + skip_gain[layer][None, :, None] * x_conv.reshape(length, HEADS, HEADDIM).astype(jnp.float32)
    gated = y_total.reshape(length, inner_width) * jax.nn.silu(gate_x[:, :inner_width].astype(jnp.float32))
    return rms_scaled(gated, out_gain[layer]).astype(jnp.bfloat16)

def reference(slide_tiles, norm_gain, in_weight, state_weight, conv_weight, conv_bias, step_bias, decay_log, skip_gain, out_gain, out_weight):
    row_count, col_count, feature_count = slide_tiles.shape
    params = (norm_gain, in_weight, state_weight, conv_weight, conv_bias, step_bias, decay_log, skip_gain, out_gain)
    first_order = jnp.transpose(slide_tiles, (1, 0, 2)).reshape(row_count * col_count, feature_count)[::-1]
    mixed_out = mixer(first_order, 0, *params)
    after_first = (first_order.astype(jnp.float32) + jnp.dot(mixed_out, out_weight[0], preferred_element_type=jnp.float32)).astype(jnp.bfloat16)
    row_grid = jnp.transpose(after_first[::-1].reshape(col_count, row_count, feature_count), (1, 0, 2))
    second = row_grid.reshape(row_count * col_count, feature_count)
    mixed_out = mixer(second, 1, *params)
    result = (second.astype(jnp.float32) + jnp.dot(mixed_out, out_weight[1], preferred_element_type=jnp.float32)).astype(jnp.bfloat16)
    return result.reshape(row_count, col_count, feature_count)
```

```python
import functools

import jax
import jax.numpy as jnp
from jax import lax
from jax.experimental import pallas as pl
from jax.experimental.pallas import tpu as pltpu
from jax.sharding import PartitionSpec as P

HEADS = 12
HEADDIM = 64
STATE = 16
GROUP = 256
EDGE = 16
EPS = 1e-05
MESH = pl.DeviceIdType.MESH
F32 = jnp.float32
BF16 = jnp.bfloat16


def silu(v):
    half = 0.5 * v
    return half + half * jnp.tanh(half)


def rms(v, gain):
    return v * lax.rsqrt(jnp.mean(v * v, axis=-1, keepdims=True) + EPS) * gain


def halves(v):
    high = v.astype(BF16)
    low = (v - high.astype(F32)).astype(BF16)
    return jnp.concatenate([high, low], axis=1)


def iota(shape, dim):
    return lax.broadcasted_iota(jnp.int32, shape, dim)


def one_hot(cond):
    return jnp.where(cond, 1.0, 0.0).astype(BF16)


def dot(a, b):
    return jnp.dot(a, b, preferred_element_type=F32)


def kernel(
    n,
    slide,
    norm_gain,
    in_hbm,
    state_weight,
    conv_weight,
    conv_bias,
    step_bias,
    decay_log,
    skip_gain,
    out_gain,
    out_hbm,
    out,
    in_w,
    out_w,
    r1,
    edge1,
    o1,
    r2,
    edge2,
    u_ref,
    x_ref,
    p_ref,
    small,
    z_ref,
    y_ref,
    grow_ref,
    c_ref,
    local_ref,
    send0,
    send1,
    gather0,
    gather1,
    arrive,
    w_sem,
    l_sem,
    s1,
    v1,
    e1s,
    e1r,
    s2,
    v2,
    e2s,
    e2r,
    g0s,
    g0r,
    g1s,
    g1r,
):
    me = lax.axis_index("seq")
    rows, cols, width = slide.shape
    full = rows * n
    block = cols // n
    tokens = rows * cols
    inner = in_hbm.shape[2] // 2
    groups = tokens // GROUP
    taps = conv_weight.shape[1]
    sources, edge = edge1.shape[0] // rows, edge1.shape[1]

    def remote(src, dst, send_sem, recv_sem, to):
        return pltpu.make_async_remote_copy(
            src_ref=src,
            dst_ref=dst,
            send_sem=send_sem,
            recv_sem=recv_sem,
            device_id={"seq": to},
            device_id_type=MESH,
        )

    weights_in = pltpu.make_async_copy(in_hbm, in_w, w_sem.at[0])
    weights_out = pltpu.make_async_copy(out_hbm, out_w, w_sem.at[1])
    weights_in.start()
    weights_out.start()

    barrier = pltpu.get_barrier_semaphore()
    for k in range(1, n):
        pl.semaphore_signal(
            barrier, inc=1, device_id={"seq": lax.rem(me + k, n)}, device_id_type=MESH
        )
    pl.semaphore_wait(barrier, n - 1)

    def at_cols(j):
        return pl.ds(pl.multiple_of(j * block, block), block)

    def at_rows(j):
        return pl.ds(j * rows, rows)

    first_copies = []
    for k in range(1, n):
        to = lax.rem(me + k, n)
        copy = remote(
            slide.at[:, at_cols(to), :], r1.at[at_rows(me)], s1.at[k - 1], v1.at[k - 1], to
        )
        copy.start()
        first_copies.append(copy)
    own = pltpu.make_async_copy(slide.at[:, at_cols(me), :], r1.at[at_rows(me)], l_sem.at[0])
    own.start()

    def edge1_copy(source, j):
        return remote(
            slide.at[:, pl.ds((j + 1) * block, edge), :],
            edge1.at[pl.ds(source * rows, rows)],
            e1s.at[j],
            e1r.at[source],
            j,
        )

    def edge1_own(source):
        return pltpu.make_async_copy(
            slide.at[:, pl.ds((source + 1) * block, edge), :],
            edge1.at[pl.ds(source * rows, rows)],
            l_sem.at[1],
        )

    for source in range(sources):

        @pl.when(me == source)
        def _():
            for j in range(n - 1):
                if j != source:
                    edge1_copy(source, j).start()
            edge1_own(source).start()

    @pl.when(me == n - 1)
    def _():
        edge1[...] = jnp.zeros_like(edge1)

    @pl.when(me == 0)
    def _():
        edge2[...] = jnp.zeros_like(edge2)

    small[...] = jnp.zeros_like(small)
    for layer in range(2):
        small[layer, 0:taps, 0 : 2 * STATE] = conv_weight[layer, :, inner : inner + 2 * STATE]
        small[layer, 4:5, 0 : 2 * STATE] = conv_bias[layer : layer + 1, inner : inner + 2 * STATE]
        small[layer, 5:6, 0:HEADS] = step_bias[layer : layer + 1, :]
        small[layer, 6:7, 0:HEADS] = decay_log[layer : layer + 1, :]
        small[layer, 7:8, 0:HEADS] = skip_gain[layer : layer + 1, :]
    p_ref[...] = jnp.zeros_like(p_ref)

    lanes = 128
    spread_row = iota((2 * lanes, inner), 0)
    spread = one_hot((spread_row % lanes) == (iota((2 * lanes, inner), 1) // HEADDIM))

    own.wait()
    for copy in first_copies:
        copy.wait_recv()
    for source in range(sources):

        @pl.when((me != source) & (me < n - 1))
        def _():
            edge1_copy(source, 0 if source else 1).wait_recv()

        @pl.when(me == source)
        def _():
            edge1_own(source).wait()

    q_of = iota((tokens, tokens), 0)
    i_of = iota((tokens, tokens), 1)
    order = one_hot(i_of == (q_of % full) * block + q_of // full)
    edge_order = one_hot(
        (iota((EDGE, edge1.shape[0] * edge), 1) == iota((EDGE, edge1.shape[0] * edge), 0) * edge)
        & (iota((EDGE, edge1.shape[0] * edge), 0) < taps - 1)
    )
    u_ref[0:tokens, :] = dot(order, r1[...].reshape(tokens, width)).astype(BF16)
    u_ref[tokens : tokens + EDGE, :] = dot(
        edge_order, edge1[...].reshape(edge1.shape[0] * edge, width)
    ).astype(BF16)

    weights_in.wait()

    def layer_out(layer, backward, sent, gathered, sends, recvs):
        base = 0 if backward else EDGE
        normed = rms(u_ref[...].astype(F32), norm_gain[layer : layer + 1, :]).astype(BF16)
        x_ref[...] = dot(normed, in_w[layer, :, inner:]).astype(BF16).astype(F32)
        z_ref[...] = dot(normed[base : base + tokens], in_w[layer, :, :inner]).astype(BF16)
        proj = dot(normed, state_weight[layer]).astype(BF16).astype(F32)
        p_ref[:, 0 : proj.shape[1]] = proj

        def shifted(ref, start, size, k):
            begin = start + (taps - 1 - k if backward else EDGE - (taps - 1) + k)
            return ref[begin : begin + size, :]

        lower = iota((GROUP, GROUP), 0) >= iota((GROUP, GROUP), 1)
        upper = iota((GROUP, GROUP), 0) <= iota((GROUP, GROUP), 1)
        allowed = upper if backward else lower
        summing = one_hot(allowed)
        narrow = iota((GROUP, lanes), 1)
        even = iota((GROUP, lanes), 1) < HEADDIM
        skip = dot(
            jnp.broadcast_to(halves(small[layer, 7:8, :]), (16, 2 * lanes)), spread
        )[0:1]
        sequence = list(range(groups))[:: -1 if backward else 1]
        last_row = 0 if backward else GROUP - 1
        carried = None
        decay = None
        for g in sequence:
            start = g * GROUP
            conv_x = jnp.broadcast_to(conv_bias[layer : layer + 1, :inner], (GROUP, inner))
            conv_p = jnp.broadcast_to(small[layer, 4:5, :], (GROUP, lanes))
            for k in range(taps):
                conv_x = conv_x + conv_weight[layer, k : k + 1, :inner] * shifted(
                    x_ref, start, GROUP, k
                )
                conv_p = conv_p + small[layer, k : k + 1, :] * shifted(p_ref, start, GROUP, k)
            xc = silu(conv_x).astype(BF16)
            bc = silu(conv_p)
            b_part = jnp.where(narrow < STATE, bc, 0.0)
            c_part = jnp.where(narrow < STATE, pltpu.roll(bc, lanes - STATE, 1), 0.0)
            b_low = b_part.astype(BF16)
            c_low = c_part.astype(BF16)
            c_ref[start : start + GROUP, :] = c_low
            raw = pltpu.roll(
                p_ref[base + start : base + start + GROUP, :], lanes - 2 * STATE, 1
            )
            raw = raw + small[layer, 5:6, :]
            step = jnp.maximum(raw, 0.0) + jnp.log1p(jnp.exp(-jnp.abs(raw)))
            step = jnp.where(narrow < HEADS, step, 0.0)
            rate = -step * jnp.exp(small[layer, 6:7, :])
            both = dot(summing, halves(rate))
            cum = both[:, :lanes] + both[:, lanes:]
            cum_rows = jnp.transpose(cum)
            grown = dot(halves(jnp.where(narrow < HEADS, jnp.exp(cum), 0.0)), spread)
            grow_ref[start : start + GROUP, :] = grown
            last = cum[last_row : last_row + 1, :]
            tail = dot(halves(jnp.exp(last - cum) * step), spread)
            stepped = dot(halves(step), spread)
            scores = lax.dot_general(
                c_low, b_low, (((1,), (1,)), ((), ())), preferred_element_type=F32
            )
            scores = jnp.where(allowed, scores, 0.0)
            xf = xc.astype(F32)
            weighted = (xf * tail).astype(BF16)
            local = dot(jnp.transpose(b_part)[0:STATE, :].astype(BF16), weighted)
            local_ref[g] = local
            grown_last = grown[last_row : last_row + 1, :]
            carried = local if carried is None else grown_last * carried + local
            decay = grown_last if decay is None else decay * grown_last
            step_x = xf * stepped
            for pair in range(HEADS // 2):
                at = slice(pair * lanes, (pair + 1) * lanes)
                xp = step_x[:, at]
                total = None
                for side in range(2):
                    h = 2 * pair + side
                    diff = jnp.minimum(cum[:, h : h + 1] - cum_rows[h : h + 1, :], 0.0)
                    weights = (scores * jnp.exp(diff)).astype(BF16)
                    masked = jnp.where(even if side == 0 else ~even, xp, 0.0).astype(BF16)
                    term = dot(weights, masked)
                    total = term if total is None else total + term
                y_ref[start : start + GROUP, at] = total + skip[:, at] * xf[:, at]

        sent[0:STATE, :] = carried.astype(BF16)
        decay_high = decay.astype(BF16).astype(F32)
        decay_rows = jnp.where(
            iota((STATE, inner), 0) == 0,
            decay_high,
            jnp.where(iota((STATE, inner), 0) == 1, decay - decay_high, 0.0),
        )
        sent[STATE : 2 * STATE, :] = decay_rows.astype(BF16)

        def state_copy(source, j):
            return remote(sent, gathered.at[source], sends.at[j], recvs.at[source], j)

        for j in range(n):

            @pl.when((me > j) if backward else (me < j))
            def _():
                state_copy(me, j).start()

        arrive[...] = jnp.zeros_like(arrive)
        for i in list(range(n))[:: -1 if backward else 1]:

            @pl.when((me < i) if backward else (me > i))
            def _():
                state_copy(i, (i + 1) % n).wait_recv()
                factor = jnp.sum(gathered[i, STATE : 2 * STATE, :].astype(F32), 0, keepdims=True)
                arrive[...] = factor * arrive[...] + gathered[i, 0:STATE, :].astype(F32)

        for j in range(n):

            @pl.when((me > j) if backward else (me < j))
            def _():
                state_copy(me, j).wait_send()

        state = arrive[...]
        results = [None] * groups
        for g in sequence:
            start = g * GROUP
            grown = grow_ref[start : start + GROUP, :]
            inter = dot(c_ref[start : start + GROUP, 0:STATE], state.astype(BF16))
            y = y_ref[start : start + GROUP, :] + grown * inter
            state = grown[last_row : last_row + 1, :] * state + local_ref[g]
            gated = y * silu(z_ref[start : start + GROUP, :].astype(F32))
            mixed = rms(gated, out_gain[layer : layer + 1, :]).astype(BF16)
            token = u_ref[base + start : base + start + GROUP, :].astype(F32)
            results[g] = (token + dot(mixed, out_w[layer])).astype(BF16)
        return jnp.concatenate(results, axis=0)

    weights_out.wait()
    after = layer_out(0, True, send0, gather0, g0s, g0r)
    back = one_hot(i_of == (q_of % block) * full + q_of // block)
    o1[...] = dot(back, after).astype(BF16).reshape(full, block, width)

    second_copies = []
    for k in range(1, n):
        to = lax.rem(me + k, n)
        copy = remote(
            o1.at[at_rows(to)], r2.at[:, at_cols(me), :], s2.at[k - 1], v2.at[k - 1], to
        )
        copy.start()
        second_copies.append(copy)
    own2 = pltpu.make_async_copy(o1.at[at_rows(me)], r2.at[:, at_cols(me), :], l_sem.at[2])
    own2.start()

    def edge2_copy(j):
        return remote(
            o1.at[rows * j - 1, pl.ds(block - edge, edge), :], edge2, e2s.at[j], e2r, j
        )

    edge2_own = pltpu.make_async_copy(
        o1.at[rows * (n - 1) - 1, pl.ds(block - edge, edge), :], edge2, l_sem.at[3]
    )

    @pl.when(me == n - 1)
    def _():
        for j in range(1, n - 1):
            edge2_copy(j).start()
        edge2_own.start()

    own2.wait()
    for copy in second_copies:
        copy.wait_recv()

    @pl.when((me > 0) & (me < n - 1))
    def _():
        edge2_copy(1).wait_recv()

    @pl.when(me == n - 1)
    def _():
        edge2_own.wait()

    if edge < EDGE:
        u_ref[0 : EDGE - edge, :] = jnp.zeros((EDGE - edge, width), BF16)
    u_ref[EDGE - edge : EDGE, :] = edge2[...]
    u_ref[EDGE : EDGE + tokens, :] = r2[...].reshape(tokens, width)
    out[...] = layer_out(1, False, send1, gather1, g1s, g1r).reshape(rows, cols, width)

    for copy in first_copies:
        copy.wait_send()
    for copy in second_copies:
        copy.wait_send()
    for source in range(sources):

        @pl.when(me == source)
        def _():
            for j in range(n - 1):
                if j != source:
                    edge1_copy(source, j).wait_send()

    @pl.when(me == n - 1)
    def _():
        for j in range(1, n - 1):
            edge2_copy(j).wait_send()


def on_device(n, *arrays):
    slide, in_weight, out_weight = arrays[0], arrays[2], arrays[10]
    rows, cols, width = slide.shape
    full, block, tokens = rows * n, cols // n, rows * cols
    inner = in_weight.shape[2] // 2
    edge = min(EDGE, block)
    sources = -(-(arrays[4].shape[1] - 1) // rows)
    vmem = pl.BlockSpec(memory_space=pltpu.VMEM)
    hbm = pl.BlockSpec(memory_space=pl.ANY)
    dma = pltpu.SemaphoreType.DMA
    return pl.pallas_call(
        functools.partial(kernel, n),
        out_shape=jax.ShapeDtypeStruct((rows, cols, width), BF16),
        in_specs=[hbm, vmem, hbm] + [vmem] * 7 + [hbm],
        out_specs=vmem,
        scratch_shapes=[
            pltpu.VMEM(in_weight.shape, BF16),
            pltpu.VMEM(out_weight.shape, BF16),
            pltpu.VMEM((full, block, width), BF16),
            pltpu.VMEM((sources * rows, edge, width), BF16),
            pltpu.VMEM((full, block, width), BF16),
            pltpu.VMEM((rows, cols, width), BF16),
            pltpu.VMEM((edge, width), BF16),
            pltpu.VMEM((tokens + EDGE, width), BF16),
            pltpu.VMEM((tokens + EDGE, inner), F32),
            pltpu.VMEM((tokens + EDGE, 128), F32),
            pltpu.VMEM((2, 8, 128), F32),
            pltpu.VMEM((tokens, inner), BF16),
            pltpu.VMEM((tokens, inner), F32),
            pltpu.VMEM((tokens, inner), F32),
            pltpu.VMEM((tokens, 128), BF16),
            pltpu.VMEM((tokens // GROUP, STATE, inner), F32),
            pltpu.VMEM((2 * STATE, inner), BF16),
            pltpu.VMEM((2 * STATE, inner), BF16),
            pltpu.VMEM((n, 2 * STATE, inner), BF16),
            pltpu.VMEM((n, 2 * STATE, inner), BF16),
            pltpu.VMEM((STATE, inner), F32),
            dma((2,)),
            dma((4,)),
            dma((n,)),
            dma((n,)),
            dma((n,)),
            dma((n,)),
            dma((n,)),
            dma((n,)),
            dma((n,)),
            dma,
            dma((n,)),
            dma((n,)),
            dma((n,)),
            dma((n,)),
        ],
        compiler_params=pltpu.CompilerParams(
            collective_id=0, has_side_effects=True, vmem_limit_bytes=60 * 1024 * 1024
        ),
    )(*arrays)


def solution(mesh):
    placed = (P(("dp", "seq"), None, None),) + (P(),) * 10
    return jax.shard_map(
        functools.partial(on_device, mesh.shape["seq"]),
        mesh=mesh,
        in_specs=placed,
        out_specs=P(("dp", "seq"), None, None),
        check_vma=False,
    )
```

```python
import functools

import jax
import jax.numpy as jnp
from jax import lax
from jax.experimental import pallas as pl
from jax.experimental.pallas import tpu as pltpu
from jax.sharding import PartitionSpec as P

HEADS = 12
HEADDIM = 64
STATE = 16
GROUP = 128
EDGE = 16
EPS = 1e-05
MESH = pl.DeviceIdType.MESH
F32 = jnp.float32
BF16 = jnp.bfloat16


def silu(v):
    half = 0.5 * v
    return half + half * jnp.tanh(half)


def rms(v, gain):
    return v * lax.rsqrt(jnp.mean(v * v, axis=-1, keepdims=True) + EPS) * gain


def halves(v):
    high = v.astype(BF16)
    low = (v - high.astype(F32)).astype(BF16)
    return jnp.concatenate([high, low], axis=1)


def iota(shape, dim):
    return lax.broadcasted_iota(jnp.int32, shape, dim)


def one_hot(cond):
    return jnp.where(cond, 1.0, 0.0).astype(BF16)


def dot(a, b):
    return jnp.dot(a, b, preferred_element_type=F32)


def kernel(
    n,
    slide,
    norm_gain,
    in_hbm,
    state_weight,
    conv_weight,
    conv_bias,
    step_bias,
    decay_log,
    skip_gain,
    out_gain,
    out_hbm,
    out,
    in_w,
    out_w,
    r1,
    edge1,
    o1,
    r2,
    edge2,
    u_ref,
    x_ref,
    p_ref,
    small,
    z_ref,
    y_ref,
    grow_ref,
    c_ref,
    xc_ref,
    step_ref,
    cum_ref,
    row_ref,
    score_ref,
    order_ref,
    back_ref,
    normed_ref,
    local_ref,
    send0,
    send1,
    gather0,
    gather1,
    arrive,
    w_sem,
    l_sem,
    s1,
    v1,
    e1s,
    e1r,
    s2,
    v2,
    e2s,
    e2r,
    g0s,
    g0r,
    g1s,
    g1r,
):
    me = lax.axis_index("seq")
    rows, cols, width = slide.shape
    full = rows * n
    block = cols // n
    tokens = rows * cols
    inner = in_hbm.shape[2] // 2
    groups = tokens // GROUP
    taps = conv_weight.shape[1]
    sources, edge = edge1.shape[0] // rows, edge1.shape[1]

    def remote(src, dst, send_sem, recv_sem, to):
        return pltpu.make_async_remote_copy(
            src_ref=src,
            dst_ref=dst,
            send_sem=send_sem,
            recv_sem=recv_sem,
            device_id={"seq": to},
            device_id_type=MESH,
        )

    weights_in = pltpu.make_async_copy(in_hbm, in_w, w_sem.at[0])
    weights_out = pltpu.make_async_copy(out_hbm, out_w, w_sem.at[1])
    weights_in.start()
    weights_out.start()

    barrier = pltpu.get_barrier_semaphore()
    for k in range(1, n):
        pl.semaphore_signal(
            barrier, inc=1, device_id={"seq": lax.rem(me + k, n)}, device_id_type=MESH
        )
    pl.semaphore_wait(barrier, n - 1)

    def at_cols(j):
        return pl.ds(pl.multiple_of(j * block, block), block)

    def at_rows(j):
        return pl.ds(j * rows, rows)

    first_copies = []
    for k in range(1, n):
        to = lax.rem(me + k, n)
        copy = remote(
            slide.at[:, at_cols(to), :], r1.at[at_rows(me)], s1.at[k - 1], v1.at[k - 1], to
        )
        copy.start()
        first_copies.append(copy)
    own = pltpu.make_async_copy(slide.at[:, at_cols(me), :], r1.at[at_rows(me)], l_sem.at[0])
    own.start()

    def edge1_copy(source, j):
        return remote(
            slide.at[:, pl.ds((j + 1) * block, edge), :],
            edge1.at[pl.ds(source * rows, rows)],
            e1s.at[j],
            e1r.at[source],
            j,
        )

    def edge1_own(source):
        return pltpu.make_async_copy(
            slide.at[:, pl.ds((source + 1) * block, edge), :],
            edge1.at[pl.ds(source * rows, rows)],
            l_sem.at[1],
        )

    for source in range(sources):

        @pl.when(me == source)
        def _():
            for j in range(n - 1):
                if j != source:
                    edge1_copy(source, j).start()
            edge1_own(source).start()

    @pl.when(me == n - 1)
    def _():
        edge1[...] = jnp.zeros_like(edge1)

    @pl.when(me == 0)
    def _():
        edge2[...] = jnp.zeros_like(edge2)

    small[...] = jnp.zeros_like(small)
    for layer in range(2):
        small[layer, 0:taps, 0 : 2 * STATE] = conv_weight[layer, :, inner : inner + 2 * STATE]
        small[layer, 4:5, 0 : 2 * STATE] = conv_bias[layer : layer + 1, inner : inner + 2 * STATE]
        small[layer, 5:6, 0:HEADS] = step_bias[layer : layer + 1, :]
        small[layer, 6:7, 0:HEADS] = decay_log[layer : layer + 1, :]
        small[layer, 7:8, 0:HEADS] = skip_gain[layer : layer + 1, :]
    p_ref[...] = jnp.zeros_like(p_ref)

    lanes = 128
    spread_row = iota((2 * lanes, inner), 0)
    spread = one_hot(jnp.bitwise_and(spread_row, lanes - 1) == iota((1, inner), 1) // HEADDIM)

    line = iota((tokens, tokens), 0)
    lane_at = iota((1, tokens), 1)
    order_ref[...] = one_hot(line == (lane_at % block) * full + lane_at // block)
    back_ref[...] = one_hot(line == (lane_at % full) * block + lane_at // full)

    own.wait()
    for copy in first_copies:
        copy.wait_recv()
    for source in range(sources):

        @pl.when((me != source) & (me < n - 1))
        def _():
            edge1_copy(source, 0 if source else 1).wait_recv()

        @pl.when(me == source)
        def _():
            edge1_own(source).wait()

    edge_order = one_hot(
        (iota((EDGE, edge1.shape[0] * edge), 1) == iota((EDGE, edge1.shape[0] * edge), 0) * edge)
        & (iota((EDGE, edge1.shape[0] * edge), 0) < taps - 1)
    )
    u_ref[0:tokens, :] = dot(order_ref[...], r1[...].reshape(tokens, width)).astype(BF16)
    u_ref[tokens : tokens + EDGE, :] = dot(
        edge_order, edge1[...].reshape(edge1.shape[0] * edge, width)
    ).astype(BF16)

    weights_in.wait()

    def layer_out(layer, backward, sent, gathered, sends, recvs):
        base = 0 if backward else EDGE
        normed = rms(u_ref[...].astype(F32), norm_gain[layer : layer + 1, :]).astype(BF16)
        x_ref[...] = dot(normed, in_w[layer, :, inner:]).astype(BF16).astype(F32)
        normed_ref[...] = normed
        proj = lax.dot_general(
            normed, state_weight[layer], (((1,), (1,)), ((), ())), preferred_element_type=F32
        )
        proj = proj.astype(BF16).astype(F32)
        p_ref[:, 0 : proj.shape[1]] = proj

        def shifted(ref, start, size, k):
            begin = start + (taps - 1 - k if backward else EDGE - (taps - 1) + k)
            return ref[begin : begin + size, :]

        lower = iota((GROUP, GROUP), 0) >= iota((GROUP, GROUP), 1)
        upper = iota((GROUP, GROUP), 0) <= iota((GROUP, GROUP), 1)
        allowed = upper if backward else lower
        summing = one_hot(allowed)
        narrow = iota((GROUP, lanes), 1)
        even = iota((GROUP, lanes), 1) < HEADDIM
        skip = dot(
            jnp.broadcast_to(halves(small[layer, 7:8, :]), (16, 2 * lanes)), spread
        )[0:1]
        sequence = list(range(groups))[:: -1 if backward else 1]
        last_row = 0 if backward else GROUP - 1
        carried = None
        decay = None
        for g in sequence:
            start = g * GROUP
            conv_x = jnp.broadcast_to(conv_bias[layer : layer + 1, :inner], (GROUP, inner))
            conv_p = jnp.broadcast_to(small[layer, 4:5, :], (GROUP, lanes))
            for k in range(taps):
                conv_x = conv_x + conv_weight[layer, k : k + 1, :inner] * shifted(
                    x_ref, start, GROUP, k
                )
                conv_p = conv_p + small[layer, k : k + 1, :] * shifted(p_ref, start, GROUP, k)
            xc = silu(conv_x).astype(BF16)
            bc = silu(conv_p)
            b_part = jnp.where(narrow < STATE, bc, 0.0)
            c_part = jnp.where(narrow < STATE, pltpu.roll(bc, lanes - STATE, 1), 0.0)
            b_low = b_part.astype(BF16)
            c_low = c_part.astype(BF16)
            c_ref[start : start + GROUP, :] = c_low
            raw = pltpu.roll(
                p_ref[base + start : base + start + GROUP, :], lanes - 2 * STATE, 1
            )
            raw = raw + small[layer, 5:6, :]
            step = jnp.maximum(raw, 0.0) + jnp.log1p(jnp.exp(-jnp.abs(raw)))
            step = jnp.where(narrow < HEADS, step, 0.0)
            rate = -step * jnp.exp(small[layer, 6:7, :])
            both = dot(summing, halves(rate))
            cum = both[:, :lanes] + both[:, lanes:]
            cum_rows = jnp.transpose(cum)
            grown = dot(halves(jnp.where(narrow < HEADS, jnp.exp(cum), 0.0)), spread)
            grow_ref[start : start + GROUP, :] = grown
            last = cum[last_row : last_row + 1, :]
            tail = dot(halves(jnp.exp(last - cum) * step), spread)
            stepped = dot(halves(step), spread)
            scores = lax.dot_general(
                c_low, b_low, (((1,), (1,)), ((), ())), preferred_element_type=F32
            )
            scores = jnp.where(allowed, scores, 0.0)
            xf = xc.astype(F32)
            weighted = (xf * tail).astype(BF16)
            local = dot(jnp.transpose(b_part)[0:STATE, :].astype(BF16), weighted)
            local_ref[g] = local
            grown_last = grown[last_row : last_row + 1, :]
            carried = local if carried is None else grown_last * carried + local
            decay = grown_last if decay is None else decay * grown_last
            step_ref[start : start + GROUP, :] = (xf * stepped).astype(BF16)
            xc_ref[start : start + GROUP, :] = xc
            cum_ref[start : start + GROUP, :] = cum
            row_ref[g] = cum_rows[0:16, :]
            score_ref[start : start + GROUP, :] = scores

        sent[0:STATE, :] = carried.astype(BF16)
        decay_high = decay.astype(BF16).astype(F32)
        decay_rows = jnp.where(
            iota((STATE, inner), 0) == 0,
            decay_high,
            jnp.where(iota((STATE, inner), 0) == 1, decay - decay_high, 0.0),
        )
        sent[STATE : 2 * STATE, :] = decay_rows.astype(BF16)

        def state_copy(source, j):
            return remote(sent, gathered.at[source], sends.at[j], recvs.at[source], j)

        for j in range(n):

            @pl.when((me > j) if backward else (me < j))
            def _():
                state_copy(me, j).start()

        z_ref[...] = dot(normed_ref[base : base + tokens, :], in_w[layer, :, :inner]).astype(BF16)
        for g in sequence:
            here = slice(g * GROUP, (g + 1) * GROUP)
            scores = score_ref[here, :]
            for pair in range(HEADS // 2):
                at = slice(pair * lanes, (pair + 1) * lanes)
                xp = step_ref[here, at]
                total = skip[:, at] * xc_ref[here, at].astype(F32)
                for side in range(2):
                    h = 2 * pair + side
                    diff = cum_ref[here, h : h + 1] - row_ref[g, h : h + 1, :]
                    weights = (scores * jnp.exp(jnp.minimum(diff, 0.0))).astype(BF16)
                    kept = even if side == 0 else ~even
                    total = total + dot(weights, jnp.where(kept, xp, jnp.zeros_like(xp)))
                y_ref[here, at] = total

        arrive[...] = jnp.zeros_like(arrive)
        for i in list(range(n))[:: -1 if backward else 1]:

            @pl.when((me < i) if backward else (me > i))
            def _():
                state_copy(i, (i + 1) % n).wait_recv()
                factor = jnp.sum(gathered[i, STATE : 2 * STATE, :].astype(F32), 0, keepdims=True)
                arrive[...] = factor * arrive[...] + gathered[i, 0:STATE, :].astype(F32)

        for j in range(n):

            @pl.when((me > j) if backward else (me < j))
            def _():
                state_copy(me, j).wait_send()

        state = arrive[...]
        results = [None] * groups
        for g in sequence:
            start = g * GROUP
            grown = grow_ref[start : start + GROUP, :]
            inter = dot(c_ref[start : start + GROUP, 0:STATE], state.astype(BF16))
            y = y_ref[start : start + GROUP, :] + grown * inter
            state = grown[last_row : last_row + 1, :] * state + local_ref[g]
            gated = y * silu(z_ref[start : start + GROUP, :].astype(F32))
            mixed = rms(gated, out_gain[layer : layer + 1, :]).astype(BF16)
            token = u_ref[base + start : base + start + GROUP, :].astype(F32)
            results[g] = (token + dot(mixed, out_w[layer])).astype(BF16)
        return jnp.concatenate(results, axis=0)

    weights_out.wait()
    after = layer_out(0, True, send0, gather0, g0s, g0r)
    o1[...] = dot(back_ref[...], after).astype(BF16).reshape(full, block, width)

    second_copies = []
    for k in range(1, n):
        to = lax.rem(me + k, n)
        copy = remote(
            o1.at[at_rows(to)], r2.at[:, at_cols(me), :], s2.at[k - 1], v2.at[k - 1], to
        )
        copy.start()
        second_copies.append(copy)
    own2 = pltpu.make_async_copy(o1.at[at_rows(me)], r2.at[:, at_cols(me), :], l_sem.at[2])
    own2.start()

    def edge2_copy(j):
        return remote(
            o1.at[rows * j - 1, pl.ds(block - edge, edge), :], edge2, e2s.at[j], e2r, j
        )

    edge2_own = pltpu.make_async_copy(
        o1.at[rows * (n - 1) - 1, pl.ds(block - edge, edge), :], edge2, l_sem.at[3]
    )

    @pl.when(me == n - 1)
    def _():
        for j in range(1, n - 1):
            edge2_copy(j).start()
        edge2_own.start()

    own2.wait()
    for copy in second_copies:
        copy.wait_recv()

    @pl.when((me > 0) & (me < n - 1))
    def _():
        edge2_copy(1).wait_recv()

    @pl.when(me == n - 1)
    def _():
        edge2_own.wait()

    if edge < EDGE:
        u_ref[0 : EDGE - edge, :] = jnp.zeros((EDGE - edge, width), BF16)
    u_ref[EDGE - edge : EDGE, :] = edge2[...]
    u_ref[EDGE : EDGE + tokens, :] = r2[...].reshape(tokens, width)
    out[...] = layer_out(1, False, send1, gather1, g1s, g1r).reshape(rows, cols, width)

    for copy in first_copies:
        copy.wait_send()
    for copy in second_copies:
        copy.wait_send()
    for source in range(sources):

        @pl.when(me == source)
        def _():
            for j in range(n - 1):
                if j != source:
                    edge1_copy(source, j).wait_send()

    @pl.when(me == n - 1)
    def _():
        for j in range(1, n - 1):
            edge2_copy(j).wait_send()


def on_device(n, *arrays):
    slide, in_weight, out_weight = arrays[0], arrays[2], arrays[10]
    rows, cols, width = slide.shape
    full, block, tokens = rows * n, cols // n, rows * cols
    inner = in_weight.shape[2] // 2
    edge = min(EDGE, block)
    sources = -(-(arrays[4].shape[1] - 1) // rows)
    vmem = pl.BlockSpec(memory_space=pltpu.VMEM)
    hbm = pl.BlockSpec(memory_space=pl.ANY)
    dma = pltpu.SemaphoreType.DMA
    return pl.pallas_call(
        functools.partial(kernel, n),
        out_shape=jax.ShapeDtypeStruct((rows, cols, width), BF16),
        in_specs=[hbm, vmem, hbm] + [vmem] * 7 + [hbm],
        out_specs=vmem,
        scratch_shapes=[
            pltpu.VMEM(in_weight.shape, BF16),
            pltpu.VMEM(out_weight.shape, BF16),
            pltpu.VMEM((full, block, width), BF16),
            pltpu.VMEM((sources * rows, edge, width), BF16),
            pltpu.VMEM((full, block, width), BF16),
            pltpu.VMEM((rows, cols, width), BF16),
            pltpu.VMEM((edge, width), BF16),
            pltpu.VMEM((tokens + EDGE, width), BF16),
            pltpu.VMEM((tokens + EDGE, inner), F32),
            pltpu.VMEM((tokens + EDGE, 128), F32),
            pltpu.VMEM((2, 8, 128), F32),
            pltpu.VMEM((tokens, inner), BF16),
            pltpu.VMEM((tokens, inner), F32),
            pltpu.VMEM((tokens, inner), F32),
            pltpu.VMEM((tokens, 128), BF16),
            pltpu.VMEM((tokens, inner), BF16),
            pltpu.VMEM((tokens, inner), BF16),
            pltpu.VMEM((tokens, 128), F32),
            pltpu.VMEM((tokens // GROUP, 16, GROUP), F32),
            pltpu.VMEM((tokens, GROUP), F32),
            pltpu.VMEM((tokens, tokens), BF16),
            pltpu.VMEM((tokens, tokens), BF16),
            pltpu.VMEM((tokens + EDGE, width), BF16),
            pltpu.VMEM((tokens // GROUP, STATE, inner), F32),
            pltpu.VMEM((2 * STATE, inner), BF16),
            pltpu.VMEM((2 * STATE, inner), BF16),
            pltpu.VMEM((n, 2 * STATE, inner), BF16),
            pltpu.VMEM((n, 2 * STATE, inner), BF16),
            pltpu.VMEM((STATE, inner), F32),
            dma((2,)),
            dma((4,)),
            dma((n,)),
            dma((n,)),
            dma((n,)),
            dma((n,)),
            dma((n,)),
            dma((n,)),
            dma((n,)),
            dma,
            dma((n,)),
            dma((n,)),
            dma((n,)),
            dma((n,)),
        ],
        compiler_params=pltpu.CompilerParams(
            collective_id=0, has_side_effects=True, vmem_limit_bytes=60 * 1024 * 1024
        ),
    )(*arrays[:3], jnp.swapaxes(arrays[3], 1, 2), *arrays[4:])


def solution(mesh):
    placed = (P(("dp", "seq"), None, None),) + (P(),) * 10
    return jax.shard_map(
        functools.partial(on_device, mesh.shape["seq"]),
        mesh=mesh,
        in_specs=placed,
        out_specs=P(("dp", "seq"), None, None),
        check_vma=False,
    )
```
